128 devices in a mesh: row: 64 (over y, z, x_lo, core), dir: 2 (over x_hi).
Axes of the slice: x: 4 (x_hi: 2, x_lo: 2; x = x_hi * 2 + x_lo), y: 4, z: 4, core: 2. Of those that a mesh axis runs over, the one named last changes fastest.
Arguments:
- incident: float32 [16384, 4096], P('row', 'dir'), may hold values from -6 to 6
- right_side: float32 [16384, 4096], P('row', 'dir'), may hold values from -6 to 6
- compress: float32 [16384, 128], P('row'), may hold values from -0.5 to 0.5
- level_diag: float32 [6, 128, 128, 128], P(None, 'row'), may hold values from -0.375 to 0.375
- level_cross: float32 [6, 128, 128, 128], P(None, 'row'), may hold values from -0.375 to 0.375
- expand: float32 [16384, 128], P('row'), may hold values from -0.5 to 0.5
- near_blocks: float32 [128, 8, 128, 128], P('row'), may hold values from -0.1875 to 0.1875
- near_cols: int32 [128, 8], P('row'), may hold values from 0 to 127, as said below
Outputs:
- residual: float32 [16384, 4096], P('row', 'dir')
- block_rms: float32 [128], P('row')
The draws below stay inside these ranges and needn't reach their ends.
Inputs may be any that keep to these rules, and one draw needn't show every extreme that they name: `near_cols`: the entries of block row b lie between max(b - 2, 0) and min(b + 2, 127), and both ends are named in every block row; entries may repeat.
All inputs are finite; a program needn't handle non-finite values.
Results may differ from the reference program's by a relative error of at most 0.0001.
Values sent between devices are 32-bit elements; how exact they have to be, the bound alone decides.
No kernel may reach another device: no remote copies, remote signals or barrier semaphores. Data moves between devices by JAX's collectives and lax.ppermute only.
A program may use at most 128 MiB of HBM per device.

```python
import jax
import jax.numpy as jnp
from jax import lax

BLK = 128
RANK = 128
NEAR = 8
BPD = 2
NBLK = 128
NROWS = 16384
COLS = 4096
LEVELS = 6


def draw_near_cols(key, part):
    offsets = jax.random.randint(jax.random.fold_in(key, 17), (NBLK, NEAR), -BPD, BPD + 1).astype(jnp.int32)
    offsets = offsets.at[:, 0].set(-BPD)
    offsets = offsets.at[:, 1].set(BPD)
    block_ids = jnp.arange(NBLK, dtype=jnp.int32)
    return jnp.clip(block_ids[:, None] + offsets, 0, NBLK - 1).astype(jnp.int32)


def shard_levels(stream_key, shape, split, least, high):
    def one(position, shards_of):
        steps = jax.random.uniform(jax.random.fold_in(jax.random.fold_in(stream_key, 6), position), (shards_of,), jnp.float32, least / len(split), high / len(split))
        return jnp.repeat(jnp.exp(steps), shape[position] // shards_of).reshape((-1,) + (1,) * (len(shape) - position - 1))

    level = one(*split[0])
    for cut in split[1:]:
        level = level * one(*cut)
    return level


def normal_values(key, dims, deviation, limit, cuts=(), kind=jnp.bfloat16):
    array = deviation * jax.random.normal(key, dims, jnp.float32)
    if cuts:
        array = array * shard_levels(key, dims, cuts, -0.22, 0.18)
    return jnp.clip(array, -limit, limit).astype(kind)


def setup_inputs(seed: int = 0) -> dict:
    streams_of = jax.random.split(jax.random.key(seed), 9)
    incident = normal_values(streams_of[0], (NROWS, COLS), 1.0, 6.0, ((0, 64), (1, 2)), jnp.float32)
    right_side = normal_values(streams_of[1], (NROWS, COLS), 1.0, 6.0, ((0, 64), (1, 2)), jnp.float32)
    compress = normal_values(streams_of[2], (NROWS, RANK), BLK ** -0.5, 0.5, ((0, 64),), jnp.float32)
    level_diag = normal_values(streams_of[3], (LEVELS, NBLK, RANK, RANK), (2 * RANK) ** -0.5, 0.375, ((1, 64),), jnp.float32)
    level_cross = normal_values(streams_of[4], (LEVELS, NBLK, RANK, RANK), (2 * RANK) ** -0.5, 0.375, ((1, 64),), jnp.float32)
    expand = normal_values(streams_of[5], (NROWS, RANK), RANK ** -0.5, 0.5, ((0, 64),), jnp.float32)
    near_blocks = normal_values(streams_of[6], (NBLK, NEAR, BLK, BLK), (NEAR * BLK) ** -0.5, 0.1875, ((0, 64),), jnp.float32)
    near_cols = draw_near_cols(jax.random.fold_in(streams_of[8], 71), 0)
    return {"incident": incident, "right_side": right_side, "compress": compress, "level_diag": level_diag, "level_cross": level_cross, "expand": expand, "near_blocks": near_blocks, "near_cols": near_cols}


def reference(incident, right_side, compress, level_diag, level_cross, expand, near_blocks, near_cols):
    highest = lax.Precision.HIGHEST
    blocks = incident.reshape(NBLK, BLK, COLS)
    coeffs = jnp.einsum('bkr,bkc->brc', compress.reshape(NBLK, BLK, RANK), blocks, precision=highest)
    block_ids = jnp.arange(NBLK, dtype=jnp.int32)
    for level_step in range(LEVELS):
        stride = BPD * 2 ** level_step
        partner = jnp.where(block_ids // stride % 2 == 0, block_ids + stride, block_ids - stride).astype(jnp.int32)
        coeffs = jnp.einsum('brs,bsc->brc', level_diag[level_step], coeffs, precision=highest) + jnp.einsum('brs,bsc->brc', level_cross[level_step], coeffs[partner], precision=highest)
    far_part = jnp.einsum('bkr,brc->bkc', expand.reshape(NBLK, BLK, RANK), coeffs, precision=highest)
    near_part = jnp.zeros((NBLK, BLK, COLS), jnp.float32)
    for near_slot in range(NEAR):
        near_part = near_part + jnp.einsum('bik,bkc->bic', near_blocks[:, near_slot], blocks[near_cols[:, near_slot]], precision=highest)
    diffs = right_side.reshape(NBLK, BLK, COLS) - far_part - near_part
    block_rms = jnp.sqrt(lax.optimization_barrier(jnp.mean(diffs * diffs, axis=(1, 2))) + 1e-06)
    return (diffs.reshape(NROWS, COLS), block_rms)
```

```python
import functools

import jax
import jax.numpy as jnp
from jax import lax
from jax.experimental import pallas as pl
from jax.experimental.pallas import tpu as pltpu
from jax.sharding import PartitionSpec as P


F32, BF16 = jnp.float32, jnp.bfloat16
WIDTHS = (256, 512, 512, 512, 256)
STARTS = (0, 512, 1024, 1536, 256)
EARLY = (0,)


def mm(a, b):
    return jnp.dot(a, b, precision=lax.Precision.HIGHEST, preferred_element_type=F32)


def split(x):
    high = x.astype(BF16)
    return high, (x - high.astype(F32)).astype(BF16)


def product(w, x):
    m = w.shape[0] // 2
    high, low = split(x)
    both = jnp.dot(w, high, preferred_element_type=F32)
    rest = jnp.dot(w[:m], low, preferred_element_type=F32)
    return both[:m] + both[m:] + rest


def put(ref, where, value):
    high, low = split(value)
    m = value.shape[0]
    ref[where + (slice(0, m),)] = high
    ref[where + (slice(m, 2 * m),)] = low


def cost(flops, size):
    return pl.CostEstimate(flops=flops, bytes_accessed=size, transcendentals=0)


def first_kernel(c, c1, d, x, out):
    b = c.shape[0] // 2
    nt = functools.partial(
        lax.dot_general,
        dimension_numbers=(((1,), (1,)), ((), ())),
        precision=lax.Precision.HIGHEST,
        preferred_element_type=F32,
    )
    for p in range(2):
        rows = slice(p * b, (p + 1) * b)
        out[p, :, :b] = nt(d[0, p], c[rows, :])
        out[p, :, b:] = nt(x[0, p], c1[rows, :])


def second_kernel(mine, other, d, x, out):
    for p in range(2):
        value = jnp.concatenate([mm(d[1, p], mine[p]), mm(x[1, p], other[p])], axis=1)
        put(out, (p,), value)


def radix4(even, d, x, o, level, p):
    d0, x0, d0o, x0o = d[level, p], x[level, p], o[0, p], o[1, p]
    d1, x1 = d[level + 1, p], x[level + 1, p]
    one, three = mm(d1, x0), mm(x1, x0o)
    return jnp.concatenate(
        [mm(d1, d0), jnp.where(even, one, three), jnp.where(even, three, one), mm(x1, d0o)], axis=1
    )


def third_kernel(place, d, x, o2, outz):
    for p in range(2):
        put(outz, (p,), radix4(place[1] == 0, d, x, o2, 2, p))


def fourth_kernel(place, d, x, o4, e, outy):
    b = e.shape[0] // 2
    for p in range(2):
        value = radix4(place[1] == 0, d, x, o4, 4, p)
        put(outy, (p,), mm(e[p * b : (p + 1) * b, :], value))


def near_weights_kernel(place, cols, blocks, out):
    i = place[0]
    odd = i % 2
    other = i + 1 - 2 * odd
    third = i - 1 + 2 * odd
    b = blocks.shape[-1]
    for p in range(2):
        for s, device in enumerate((i, other, third)):
            for q in range(2):
                wanted = 2 * device + q
                total = jnp.zeros((b, b), F32)
                for j in range(blocks.shape[1]):
                    total = total + jnp.where(cols[p, j] == wanted, blocks[p, j], 0.0)
                high, low = split(total)
                k = (2 * s + q) * b
                out[p * b : (p + 1) * b, k : k + b] = high
                out[(2 + p) * b : (3 + p) * b, k : k + b] = low


def stage_x_kernel(start, w, own, one, two, three, out):
    width = out.shape[1]
    b = out.shape[0] // 2
    for p in range(2):
        rows = slice(p * b, (p + 1) * b)
        x = jnp.concatenate(
            [own[rows, :], one[rows, start : start + width], two[rows, :], three[rows, :]], axis=0
        )
        out[rows, :] = product(w[p], x)


def stage_z_kernel(w, own, a, b, c, out):
    n = out.shape[0] // 2
    for p in range(2):
        rows = slice(p * n, (p + 1) * n)
        x = jnp.concatenate([ref[rows, :] for ref in (own, a, b, c)], axis=0)
        out[rows, :] = product(w[p], x)


def near_kernel(start, place, w, own, one, three, halo, right, out):
    here = slice(start, start + out.shape[1])
    third = jnp.where(place[2] == 1, halo[...], three[...])
    x = jnp.concatenate([own[...], one[:, here], third], axis=0)
    out[...] = right[:, here] - product(w[...], x)


def last_kernel(w, own, a, b, c, part, *refs):
    old_sum, out, total = refs[-3:]
    n = out.shape[0] // 2
    for p in range(2):
        rows = slice(p * n, (p + 1) * n)
        x = jnp.concatenate([ref[rows, :] for ref in (own, a, b, c)], axis=0)
        diff = part[rows, :] - product(w[p], x)
        out[rows, :] = diff
        total[p : p + 1, :] = old_sum[p : p + 1, :] + jnp.full((1, 128), jnp.sum(diff * diff), F32)


def xor(x, bits, odd_bits=None):
    count = lax.axis_size("row")
    odd_bits = bits if odd_bits is None else odd_bits
    return lax.ppermute(x, "row", [(i, i ^ (odd_bits if i % 2 else bits)) for i in range(count)])


def halo_of(x, two, early):
    count = lax.axis_size("row")
    if early:
        route = [(i, i + 1) for i in range(3, count - 1, 4)]
        return lax.ppermute(x, "row", route + [(j, i) for i, j in route])
    route = [(i, i + 3) for i in range(1, count - 3, 4)] + [(i, i - 3) for i in range(6, count, 4)]
    return lax.ppermute(two, "row", route)


VM = pl.BlockSpec(memory_space=pltpu.VMEM)
SM = pl.BlockSpec(memory_space=pltpu.SMEM)
ANY = pl.BlockSpec(memory_space=pl.ANY)


def call(kernel, in_specs, out_shape, flops, *args, limit=6, **kwargs):
    size = sum(a.size * a.dtype.itemsize for a in args)
    kwargs.setdefault("out_specs", VM)
    return pl.pallas_call(
        kernel,
        in_specs=in_specs,
        out_shape=out_shape,
        cost_estimate=cost(flops, size // 4),
        compiler_params=pltpu.CompilerParams(vmem_limit_bytes=limit * 2**20),
        **kwargs,
    )(*args)


def shards(incident, right_side, compress, level_diag, level_cross, expand, near_blocks, near_cols):
    rows, cols = incident.shape
    b = near_blocks.shape[2]
    i = lax.axis_index("row")
    quad = i % 4
    place = jnp.stack([i, i % 2, ((quad == 0) | (quad == 3)).astype(jnp.int32)]).astype(jnp.int32)
    shape = jax.ShapeDtypeStruct
    weights = shape((2, 2 * b, 4 * b), BF16)

    comp1 = xor(compress, 1)
    raw = [lax.slice_in_dim(incident, s, s + w, axis=1) for s, w in zip(STARTS, WIDTHS)]
    two = [xor(x, 2) for x in raw]
    one = xor(incident, 1)
    mine = call(
        first_kernel, [VM] * 4, shape((2, b, 2 * b), F32), 48 * b**3,
        compress, comp1, level_diag, level_cross,
    )
    ends = [(i * 2 + d, (i ^ 2) * 2 + 1 - d) for i in range(lax.axis_size("row")) for d in range(2)]
    theirs = lax.ppermute(mine, ("row", "dir"), ends)
    pair = lambda level: jnp.stack([level_diag[level], level_cross[level]])
    o2 = xor(pair(2), 8)
    o4 = xor(pair(4), 32)
    wx = call(second_kernel, [VM] * 4, weights, 96 * b**3, mine, theirs, level_diag, level_cross)
    wn = call(
        near_weights_kernel, [SM, SM, VM], shape((4 * b, 6 * b), BF16), 2**22,
        place, near_cols, near_blocks,
    )
    wz = call(third_kernel, [SM] + [VM] * 3, weights, 96 * b**3, place, level_diag, level_cross, o2)
    wy = call(
        fourth_kernel, [SM] + [VM] * 4, weights, 200 * b**3,
        place, level_diag, level_cross, o4, expand,
    )

    def gathered(x, near_bits, far_bits):
        a = xor(x, near_bits, far_bits)
        c = xor(x, far_bits, near_bits)
        return x, a, c, xor(a, far_bits, near_bits)

    result = None
    total = jnp.zeros((2, 128), F32)
    for k, (s, w) in enumerate(zip(STARTS, WIDTHS)):
        flops = 2 * 3 * 2 * 4 * b * b * w
        piece = shape((rows, w), F32)
        three = xor(two[k], 1)
        halo = halo_of(raw[k], two[k], k in EARLY)
        coeffs = call(functools.partial(stage_x_kernel, s), [VM] * 5, piece, flops, wx, raw[k], one, two[k], three)
        coeffs = call(stage_z_kernel, [VM] * 5, piece, flops, wz, *gathered(coeffs, 4, 12))
        part = call(
            functools.partial(near_kernel, s), [SM] + [VM] * 6, piece, 2 * flops,
            place, wn, raw[k], one, three, halo, right_side,
        )
        ins = gathered(coeffs, 16, 48)
        olds = () if result is None else (result,)
        out = pl.BlockSpec((rows, w), lambda j, s=s // w: (0, s))
        result, total = call(
            last_kernel, [VM] * 6 + [ANY] * len(olds) + [VM],
            [shape((rows, cols), F32), shape((2, 128), F32)], flops,
            wy, *ins, part, *olds, total,
            grid=(1,), out_specs=[out, VM],
            input_output_aliases={6: 0} if olds else {},
        )

    mate = lax.ppermute(total, "dir", [(0, 1), (1, 0)])
    mean = (total[:, 0] + mate[:, 0]) / (b * cols * lax.axis_size("dir"))
    return result, jnp.sqrt(mean + 1e-06)


def solution(mesh):
    return jax.shard_map(
        shards,
        mesh=mesh,
        in_specs=(
            P("row", "dir"),
            P("row", "dir"),
            P("row", None),
            P(None, "row", None, None),
            P(None, "row", None, None),
            P("row", None),
            P("row", None, None, None),
            P("row", None),
        ),
        out_specs=(P("row", "dir"), P("row")),
        check_vma=False,
    )
```

```python
import functools

import jax
import jax.numpy as jnp
from jax import lax
from jax.experimental import pallas as pl
from jax.experimental.pallas import tpu as pltpu
from jax.sharding import PartitionSpec as P


F32, BF16 = jnp.float32, jnp.bfloat16
WIDTHS = (256, 512, 512, 512, 256)
STARTS = (0, 512, 1024, 1536, 256)


def mm(a, b):
    return jnp.dot(a, b, precision=lax.Precision.HIGHEST, preferred_element_type=F32)


def split(x):
    high = x.astype(BF16)
    return high, (x - high.astype(F32)).astype(BF16)


def product(w, x):
    m = w.shape[0] // 2
    high, low = split(x)
    both = jnp.dot(w, high, preferred_element_type=F32)
    rest = jnp.dot(w[:m], low, preferred_element_type=F32)
    return both[:m] + both[m:] + rest


def put(ref, where, value):
    high, low = split(value)
    m = value.shape[0]
    ref[where + (slice(0, m),)] = high
    ref[where + (slice(m, 2 * m),)] = low


def cost(flops, size):
    return pl.CostEstimate(flops=flops, bytes_accessed=size, transcendentals=0)


def copy_kernel(x, out):
    out[...] = x[...]


def pairs_kernel(d2, x2, d4, x4, out2, out4):
    out2[0] = d2[0]
    out2[1] = x2[0]
    out4[0] = d4[0]
    out4[1] = x4[0]


def first_kernel(c, c1, d, x, out):
    b = c.shape[0] // 2
    nt = functools.partial(
        lax.dot_general,
        dimension_numbers=(((1,), (1,)), ((), ())),
        precision=lax.Precision.HIGHEST,
        preferred_element_type=F32,
    )
    for p in range(2):
        rows = slice(p * b, (p + 1) * b)
        out[p, :, :b] = nt(d[0, p], c[rows, :])
        out[p, :, b:] = nt(x[0, p], c1[rows, :])


def second_kernel(mine, other, d, x, out):
    for p in range(2):
        value = jnp.concatenate([mm(d[1, p], mine[p]), mm(x[1, p], other[p])], axis=1)
        put(out, (p,), value)


def radix4(even, d, x, o, level, p):
    d0, x0, d0o, x0o = d[level, p], x[level, p], o[0, p], o[1, p]
    d1, x1 = d[level + 1, p], x[level + 1, p]
    one, three = mm(d1, x0), mm(x1, x0o)
    return jnp.concatenate(
        [mm(d1, d0), jnp.where(even, one, three), jnp.where(even, three, one), mm(x1, d0o)], axis=1
    )


def third_kernel(place, d, x, o2, outz):
    for p in range(2):
        put(outz, (p,), radix4(place[1] == 0, d, x, o2, 2, p))


def fourth_kernel(place, d, x, o4, e, outy):
    b = e.shape[0] // 2
    for p in range(2):
        value = radix4(place[1] == 0, d, x, o4, 4, p)
        put(outy, (p,), mm(e[p * b : (p + 1) * b, :], value))


def near_weights_kernel(place, cols, blocks, out):
    i = place[0]
    odd = i % 2
    other = i + 1 - 2 * odd
    third = i - 1 + 2 * odd
    b = blocks.shape[-1]
    for p in range(2):
        for s, device in enumerate((i, other, third)):
            for q in range(2):
                wanted = 2 * device + q
                total = jnp.zeros((b, b), F32)
                for j in range(blocks.shape[1]):
                    total = total + jnp.where(cols[p, j] == wanted, blocks[p, j], 0.0)
                high, low = split(total)
                k = (2 * s + q) * b
                out[p * b : (p + 1) * b, k : k + b] = high
                out[(2 + p) * b : (3 + p) * b, k : k + b] = low


def stage_x_kernel(start, w, own, one, two, three, out):
    width = out.shape[1]
    b = out.shape[0] // 2
    for p in range(2):
        rows = slice(p * b, (p + 1) * b)
        x = jnp.concatenate(
            [own[rows, :], one[rows, start : start + width], two[rows, :], three[rows, :]], axis=0
        )
        out[rows, :] = product(w[p], x)


def stage_z_kernel(w, own, a, b, c, out):
    n = out.shape[0] // 2
    for p in range(2):
        rows = slice(p * n, (p + 1) * n)
        x = jnp.concatenate([ref[rows, :] for ref in (own, a, b, c)], axis=0)
        out[rows, :] = product(w[p], x)


def near_kernel(start, place, w, own, one, three, halo, cross, right, out):
    here = slice(start, start + out.shape[1])
    third = jnp.where(place[2] == 1, halo[...] + cross[...], three[...])
    x = jnp.concatenate([own[...], one[:, here], third], axis=0)
    out[...] = right[:, here] - product(w[...], x)


def last_kernel(w, own, a, b, c, part, *refs):
    old_sum, out, total = refs[-3:]
    n = out.shape[0] // 2
    for p in range(2):
        rows = slice(p * n, (p + 1) * n)
        x = jnp.concatenate([ref[rows, :] for ref in (own, a, b, c)], axis=0)
        diff = part[rows, :] - product(w[p], x)
        out[rows, :] = diff
        total[p : p + 1, :] = old_sum[p : p + 1, :] + jnp.full((1, 128), jnp.sum(diff * diff), F32)


def xor(x, bits, odd_bits=None):
    count = lax.axis_size("row")
    odd_bits = bits if odd_bits is None else odd_bits
    return lax.ppermute(x, "row", [(i, i ^ (odd_bits if i % 2 else bits)) for i in range(count)])


def halo_of(two, crossing):
    count = lax.axis_size("row")
    route = [(i, i + 3) for i in range(1, count - 3, 4)]
    route = [(i, j) for i, j in route if (i // 16 != j // 16) == crossing]
    return lax.ppermute(two, "row", route + [(j + 2, i + 2) for i, j in route])


VM = pl.BlockSpec(memory_space=pltpu.VMEM)
SM = pl.BlockSpec(memory_space=pltpu.SMEM)
ANY = pl.BlockSpec(memory_space=pl.ANY)


def call(kernel, in_specs, out_shape, flops, *args, limit=6, **kwargs):
    size = sum(a.size * a.dtype.itemsize for a in args)
    kwargs.setdefault("out_specs", VM)
    return pl.pallas_call(
        kernel,
        in_specs=in_specs,
        out_shape=out_shape,
        cost_estimate=cost(flops, size // 4),
        compiler_params=pltpu.CompilerParams(vmem_limit_bytes=limit * 2**20),
        **kwargs,
    )(*args)


def shards(incident, right_side, compress, level_diag, level_cross, expand, near_blocks, near_cols):
    rows, cols = incident.shape
    b = near_blocks.shape[2]
    i = lax.axis_index("row")
    quad = i % 4
    place = jnp.stack([i, i % 2, ((quad == 0) | (quad == 3)).astype(jnp.int32)]).astype(jnp.int32)
    shape = jax.ShapeDtypeStruct
    weights = shape((2, 2 * b, 4 * b), BF16)

    comp1 = xor(compress, 1)
    raw = [
        call(
            copy_kernel, [pl.BlockSpec((rows, w), lambda j, s=s // w: (0, s))],
            shape((rows, w), F32), 0, incident, grid=(1,),
        )
        for s, w in zip(STARTS, WIDTHS)
    ]
    two = [xor(x, 2) for x in raw]
    one = xor(incident, 1)
    mine = call(
        first_kernel, [VM] * 4, shape((2, b, 2 * b), F32), 48 * b**3,
        compress, comp1, level_diag, level_cross,
    )
    ends = [(i * 2 + d, (i ^ 2) * 2 + 1 - d) for i in range(lax.axis_size("row")) for d in range(2)]
    theirs = lax.ppermute(mine, ("row", "dir"), ends)
    pairs = shape((2, 2, b, b), F32)
    levels = [pl.BlockSpec((1, 2, b, b), lambda j, q=q: (q, 0, 0, 0)) for q in (2, 2, 4, 4)]
    pair2, pair4 = call(
        pairs_kernel, levels, [pairs, pairs], 0,
        level_diag, level_cross, level_diag, level_cross, grid=(1,), out_specs=[VM, VM],
    )
    o2 = xor(pair2, 8)
    o4 = xor(pair4, 32)
    wx = call(second_kernel, [VM] * 4, weights, 96 * b**3, mine, theirs, level_diag, level_cross)
    wn = call(
        near_weights_kernel, [SM, SM, VM], shape((4 * b, 6 * b), BF16), 2**22,
        place, near_cols, near_blocks,
    )
    wz = call(third_kernel, [SM] + [VM] * 3, weights, 96 * b**3, place, level_diag, level_cross, o2)
    wy = call(
        fourth_kernel, [SM] + [VM] * 4, weights, 200 * b**3,
        place, level_diag, level_cross, o4, expand,
    )

    def gathered(x, near_bits, far_bits):
        a = xor(x, near_bits, far_bits)
        c = xor(x, far_bits, near_bits)
        return x, a, c, xor(a, far_bits, near_bits)

    result = None
    total = jnp.zeros((2, 128), F32)
    for k, (s, w) in enumerate(zip(STARTS, WIDTHS)):
        flops = 2 * 3 * 2 * 4 * b * b * w
        piece = shape((rows, w), F32)
        three = xor(two[k], 1)
        halo = halo_of(two[k], False)
        cross = halo_of(two[k], True)
        coeffs = call(functools.partial(stage_x_kernel, s), [VM] * 5, piece, flops, wx, raw[k], one, two[k], three)
        coeffs = call(stage_z_kernel, [VM] * 5, piece, flops, wz, *gathered(coeffs, 4, 12))
        part = call(
            functools.partial(near_kernel, s), [SM] + [VM] * 7, piece, 2 * flops,
            place, wn, raw[k], one, three, halo, cross, right_side,
        )
        ins = gathered(coeffs, 16, 48)
        olds = () if result is None else (result,)
        out = pl.BlockSpec((rows, w), lambda j, s=s // w: (0, s))
        result, total = call(
            last_kernel, [VM] * 6 + [ANY] * len(olds) + [VM],
            [shape((rows, cols), F32), shape((2, 128), F32)], flops,
            wy, *ins, part, *olds, total,
            grid=(1,), out_specs=[out, VM],
            input_output_aliases={6: 0} if olds else {},
        )

    mate = lax.ppermute(total, "dir", [(0, 1), (1, 0)])
    mean = (total[:, 0] + mate[:, 0]) / (b * cols * lax.axis_size("dir"))
    return result, jnp.sqrt(mean + 1e-06)


def solution(mesh):
    return jax.shard_map(
        shards,
        mesh=mesh,
        in_specs=(
            P("row", "dir"),
            P("row", "dir"),
            P("row", None),
            P(None, "row", None, None),
            P(None, "row", None, None),
            P("row", None),
            P("row", None, None, None),
            P("row", None),
        ),
        out_specs=(P("row", "dir"), P("row")),
        check_vma=False,
    )
```

```python
import functools

import jax
import jax.numpy as jnp
from jax import lax
from jax.experimental import pallas as pl
from jax.experimental.pallas import tpu as pltpu
from jax.sharding import PartitionSpec as P


F32, BF16 = jnp.float32, jnp.bfloat16
WIDTHS = (256, 512, 512, 384, 384)
STARTS = (768, 1024, 1536, 0, 384)
SPLIT = (1, 2)


def mm(a, b):
    return jnp.dot(a, b, precision=lax.Precision.HIGHEST, preferred_element_type=F32)


def split(x):
    high = x.astype(BF16)
    return high, (x - high.astype(F32)).astype(BF16)


def product(w, x):
    m = w.shape[0] // 2
    high, low = split(x)
    both = jnp.dot(w, high, preferred_element_type=F32)
    rest = jnp.dot(w[:m], low, preferred_element_type=F32)
    return both[:m] + both[m:] + rest


def put(ref, where, value):
    high, low = split(value)
    m = value.shape[0]
    ref[where + (slice(0, m),)] = high
    ref[where + (slice(m, 2 * m),)] = low


def cost(flops, size):
    return pl.CostEstimate(flops=flops, bytes_accessed=size, transcendentals=0)


def copy_kernel(x, out):
    out[...] = x[...]


def pairs_kernel(d2, x2, d4, x4, out2, out4):
    out2[0] = d2[0]
    out2[1] = x2[0]
    out4[0] = d4[0]
    out4[1] = x4[0]


def first_kernel(c, c1, d, x, out):
    b = c.shape[0] // 2
    nt = functools.partial(
        lax.dot_general,
        dimension_numbers=(((1,), (1,)), ((), ())),
        precision=lax.Precision.HIGHEST,
        preferred_element_type=F32,
    )
    for p in range(2):
        rows = slice(p * b, (p + 1) * b)
        out[p, :, :b] = nt(d[0, p], c[rows, :])
        out[p, :, b:] = nt(x[0, p], c1[rows, :])


def second_kernel(mine, other, d, x, out):
    for p in range(2):
        value = jnp.concatenate([mm(d[1, p], mine[p]), mm(x[1, p], other[p])], axis=1)
        put(out, (p,), value)


def radix4(even, d, x, o, level, p):
    d0, x0, d0o, x0o = d[level, p], x[level, p], o[0, p], o[1, p]
    d1, x1 = d[level + 1, p], x[level + 1, p]
    one, three = mm(d1, x0), mm(x1, x0o)
    return jnp.concatenate(
        [mm(d1, d0), jnp.where(even, one, three), jnp.where(even, three, one), mm(x1, d0o)], axis=1
    )


def third_kernel(place, d, x, o2, outz):
    for p in range(2):
        put(outz, (p,), radix4(place[1] == 0, d, x, o2, 2, p))


def fourth_kernel(place, d, x, o4, e, outy):
    b = e.shape[0] // 2
    for p in range(2):
        value = radix4(place[1] == 0, d, x, o4, 4, p)
        put(outy, (p,), mm(e[p * b : (p + 1) * b, :], value))


def near_weights_kernel(place, cols, blocks, out):
    i = place[0]
    odd = i % 2
    other = i + 1 - 2 * odd
    third = i - 1 + 2 * odd
    b = blocks.shape[-1]
    for p in range(2):
        for s, device in enumerate((i, other, third)):
            for q in range(2):
                wanted = 2 * device + q
                total = jnp.zeros((b, b), F32)
                for j in range(blocks.shape[1]):
                    total = total + jnp.where(cols[p, j] == wanted, blocks[p, j], 0.0)
                high, low = split(total)
                k = (2 * s + q) * b
                out[p * b : (p + 1) * b, k : k + b] = high
                out[(2 + p) * b : (3 + p) * b, k : k + b] = low


def stage_x_kernel(start, w, own, one, two, three, out):
    width = out.shape[1]
    b = out.shape[0] // 2
    for p in range(2):
        rows = slice(p * b, (p + 1) * b)
        x = jnp.concatenate(
            [own[rows, :], one[rows, start : start + width], two[rows, :], three[rows, :]], axis=0
        )
        out[rows, :] = product(w[p], x)


def stage_z_kernel(w, own, a, b, c, out):
    n = out.shape[0] // 2
    for p in range(2):
        rows = slice(p * n, (p + 1) * n)
        x = jnp.concatenate([ref[rows, :] for ref in (own, a, b, c)], axis=0)
        out[rows, :] = product(w[p], x)


def near_kernel(start, place, w, own, one, three, halo, *refs):
    right, out = refs[-2:]
    here = slice(start, start + out.shape[1])
    edge = halo[...] + refs[0][...] if len(refs) == 3 else halo[...]
    third = jnp.where(place[2] == 1, edge, three[...])
    x = jnp.concatenate([own[...], one[:, here], third], axis=0)
    out[...] = right[:, here] - product(w[...], x)


def last_kernel(w, own, a, b, c, part, *refs):
    old_sum, out, total = refs[-3:]
    n = out.shape[0] // 2
    for p in range(2):
        rows = slice(p * n, (p + 1) * n)
        x = jnp.concatenate([ref[rows, :] for ref in (own, a, b, c)], axis=0)
        diff = part[rows, :] - product(w[p], x)
        out[rows, :] = diff
        total[p : p + 1, :] = old_sum[p : p + 1, :] + jnp.full((1, 128), jnp.sum(diff * diff), F32)


def xor(x, bits, odd_bits=None):
    count = lax.axis_size("row")
    odd_bits = bits if odd_bits is None else odd_bits
    return lax.ppermute(x, "row", [(i, i ^ (odd_bits if i % 2 else bits)) for i in range(count)])


def halo_of(k, two, three, part):
    count = lax.axis_size("row")
    ends = [(i, i + 1) for i in range(3, count - 1, 4)]
    if part is not None:
        ends = [(i, j) for i, j in ends if (i // 16 != j // 16) == part]
    odd = k % 2
    route = [((i ^ 3) if odd else (i ^ 2), j) for i, j in ends]
    route += [((j ^ 3) if odd else (j ^ 2), i) for i, j in ends]
    return lax.ppermute(three if odd else two, "row", route)


VM = pl.BlockSpec(memory_space=pltpu.VMEM)
SM = pl.BlockSpec(memory_space=pltpu.SMEM)
ANY = pl.BlockSpec(memory_space=pl.ANY)


def call(kernel, in_specs, out_shape, flops, *args, limit=6, **kwargs):
    size = sum(a.size * a.dtype.itemsize for a in args)
    kwargs.setdefault("out_specs", VM)
    return pl.pallas_call(
        kernel,
        in_specs=in_specs,
        out_shape=out_shape,
        cost_estimate=cost(flops, size // 4),
        compiler_params=pltpu.CompilerParams(vmem_limit_bytes=limit * 2**20),
        **kwargs,
    )(*args)


def shards(incident, right_side, compress, level_diag, level_cross, expand, near_blocks, near_cols):
    rows, cols = incident.shape
    b = near_blocks.shape[2]
    i = lax.axis_index("row")
    quad = i % 4
    place = jnp.stack([i, i % 2, ((quad == 0) | (quad == 3)).astype(jnp.int32)]).astype(jnp.int32)
    shape = jax.ShapeDtypeStruct
    weights = shape((2, 2 * b, 4 * b), BF16)

    comp1 = xor(compress, 1)
    raw = [
        call(
            copy_kernel, [pl.BlockSpec((rows, w), lambda j, s=s // w: (0, s))],
            shape((rows, w), F32), 0, incident, grid=(1,),
        )
        for s, w in zip(STARTS, WIDTHS)
    ]
    two = [xor(x, 2) for x in raw]
    one = xor(incident, 1)
    mine = call(
        first_kernel, [VM] * 4, shape((2, b, 2 * b), F32), 48 * b**3,
        compress, comp1, level_diag, level_cross,
    )
    ends = [(i * 2 + d, (i ^ 2) * 2 + 1 - d) for i in range(lax.axis_size("row")) for d in range(2)]
    theirs = lax.ppermute(mine, ("row", "dir"), ends)
    pairs = shape((2, 2, b, b), F32)
    levels = [pl.BlockSpec((1, 2, b, b), lambda j, q=q: (q, 0, 0, 0)) for q in (2, 2, 4, 4)]
    pair2, pair4 = call(
        pairs_kernel, levels, [pairs, pairs], 0,
        level_diag, level_cross, level_diag, level_cross, grid=(1,), out_specs=[VM, VM],
    )
    o2 = xor(pair2, 8)
    o4 = xor(pair4, 32)
    wx = call(second_kernel, [VM] * 4, weights, 96 * b**3, mine, theirs, level_diag, level_cross)
    wn = call(
        near_weights_kernel, [SM, SM, VM], shape((4 * b, 6 * b), BF16), 2**22,
        place, near_cols, near_blocks,
    )
    wz = call(third_kernel, [SM] + [VM] * 3, weights, 96 * b**3, place, level_diag, level_cross, o2)
    wy = call(
        fourth_kernel, [SM] + [VM] * 4, weights, 200 * b**3,
        place, level_diag, level_cross, o4, expand,
    )

    def gathered(x, near_bits, far_bits):
        a = xor(x, near_bits, far_bits)
        c = xor(x, far_bits, near_bits)
        return x, a, c, xor(a, far_bits, near_bits)

    result = None
    total = jnp.zeros((2, 128), F32)
    for k, (s, w) in enumerate(zip(STARTS, WIDTHS)):
        flops = 2 * 3 * 2 * 4 * b * b * w
        piece = shape((rows, w), F32)
        three = xor(two[k], 1)
        halo = halo_of(k, two[k], three, False if k in SPLIT else None)
        cross = halo_of(k, two[k], three, True) if k in SPLIT else None
        coeffs = call(functools.partial(stage_x_kernel, s), [VM] * 5, piece, flops, wx, raw[k], one, two[k], three)
        coeffs = call(stage_z_kernel, [VM] * 5, piece, flops, wz, *gathered(coeffs, 4, 12))
        part = call(
            functools.partial(near_kernel, s), [SM] + [VM] * (7 if k in SPLIT else 6), piece, 2 * flops,
            *([place, wn, raw[k], one, three, halo] + ([cross] if k in SPLIT else []) + [right_side]),
        )
        ins = gathered(coeffs, 16, 48)
        olds = () if result is None else (result,)
        out = pl.BlockSpec((rows, w), lambda j, s=s // w: (0, s))
        result, total = call(
            last_kernel, [VM] * 6 + [ANY] * len(olds) + [VM],
            [shape((rows, cols), F32), shape((2, 128), F32)], flops,
            wy, *ins, part, *olds, total,
            grid=(1,), out_specs=[out, VM],
            input_output_aliases={6: 0} if olds else {},
        )

    mate = lax.ppermute(total, "dir", [(0, 1), (1, 0)])
    mean = (total[:, 0] + mate[:, 0]) / (b * cols * lax.axis_size("dir"))
    return result, jnp.sqrt(mean + 1e-06)


def solution(mesh):
    return jax.shard_map(
        shards,
        mesh=mesh,
        in_specs=(
            P("row", "dir"),
            P("row", "dir"),
            P("row", None),
            P(None, "row", None, None),
            P(None, "row", None, None),
            P("row", None),
            P("row", None, None, None),
            P("row", None),
        ),
        out_specs=(P("row", "dir"), P("row")),
        check_vma=False,
    )
```
